32 devices in a mesh: mem: 4 (over z), tile: 8 (over y, x, core).
Axes of the slice: x: 2, y: 2, z: 4, core: 2. Of those that a mesh axis runs over, the one named last changes fastest.
Arguments:
- state: float32 [20, 8, 12960], P('mem', 'tile'), may hold values from -6 to 6
- obs_index: int32 [8, 256], P('tile'), may hold values from 0 to 12959
- obs_count: int32 [8], P('tile'), may hold values from 32 to 256, as said below
- obs_value: float32 [8, 256], P('tile'), may hold values from -8 to 8
- obs_rinv: float32 [8, 256], P('tile'), may hold values from 0.1 to 1
- radius: int32 [8], P('tile'), may hold values from 1 to 2
Outputs:
- analysis: float32 [20, 8, 12960], P('mem', 'tile')
The draws below stay inside these ranges and needn't reach their ends.
Inputs may be any that keep to these rules, and one draw needn't show every extreme that they name: `obs_count`: at most 256; some tile has exactly 256 in every draw.
All inputs are finite; a program needn't handle non-finite values.
Results may differ from the reference program's by a relative error of at most 0.0003.
Values sent between devices are 32-bit elements; how exact they have to be, the bound alone decides.
A program may use at most 64 MiB of HBM per device.

```python
import math
import jax
import jax.numpy as jnp
from jax import lax

LAT = 288
COLS = 45
BLOCK = 9
SLOTS = 256
HALO = 2
NS_ITERS = 4
MEMBERS = 20
TILES = 8
CELLS_TILE = 12960
N_MEM = 4


def draw_obs_count(key, part):
    base_key = jax.random.fold_in(key, 11)
    order_key = jax.random.fold_in(key, 12)
    base = jax.random.randint(base_key, (TILES,), SLOTS // 8, SLOTS // 3 + 1)
    order = jax.random.permutation(order_key, TILES)
    dense = order < max(1, TILES // 8)
    return jnp.where(dense, SLOTS, base).astype(jnp.int32)


def plant(array, own_key, low, high):
    spot = [jax.random.randint(jax.random.fold_in(own_key, axis), (), 0, length) for axis, length in enumerate(array.shape)]
    widest = array.shape.index(max(array.shape))
    neighbour = spot[:widest] + [(spot[widest] + 1) % array.shape[widest]] + spot[widest + 1:]
    return array.at[tuple(spot)].set(low).at[tuple(neighbour)].set(high)


def block_scale(key, shape, pieces, low, top_value):
    factor_of, own = 1.0, jax.random.fold_in(key, 6)
    for axis_at, shards_of in pieces:
        draws = jnp.exp(jax.random.uniform(jax.random.fold_in(own, axis_at), (shards_of,), jnp.float32, low / len(pieces), top_value / len(pieces)))
        factor_of = factor_of * jnp.repeat(draws, shape[axis_at] // shards_of).reshape([-1 if axis == axis_at else 1 for axis in range(len(shape))])
    return factor_of


def gaussian(own_key, dims, width, most, split=(), held_as=jnp.bfloat16):
    factor_of = block_scale(own_key, dims, split, -0.22, 0.18) if split else 1.0
    entries = jax.random.normal(own_key, dims, jnp.float32) * width * factor_of
    return jnp.minimum(jnp.maximum(entries, -most), most).astype(held_as)


def setup_inputs(seed: int = 0) -> dict:
    arg_keys = jax.random.split(jax.random.key(seed), 7)
    state = gaussian(arg_keys[0], (MEMBERS, TILES, CELLS_TILE), 1.0, 6.0, ((0, 4), (1, 8)), jnp.float32)
    obs_index = plant(jax.random.randint(arg_keys[1], (TILES, SLOTS), 0, LAT * COLS), jax.random.fold_in(arg_keys[1], 1), 0, (LAT * COLS) - 1).astype(jnp.int32)
    obs_count = draw_obs_count(jax.random.fold_in(arg_keys[6], 71), 0)
    obs_value = gaussian(arg_keys[3], (TILES, SLOTS), 1.5, 8.0, ((0, 8),), jnp.float32)
    obs_rinv = jnp.clip(jnp.exp(math.log(1.0) - 2.3025851 * jax.random.uniform(arg_keys[4], (TILES, SLOTS), jnp.float32) ** block_scale(arg_keys[4], (TILES, SLOTS), ((0, 8),), -0.2, 0.2)), 0.1, 1.0)
    radius = plant(jax.random.randint(arg_keys[5], (TILES,), 1, HALO + 1), jax.random.fold_in(arg_keys[5], 1), 1, HALO).astype(jnp.int32)
    return {"state": state, "obs_index": obs_index, "obs_count": obs_count, "obs_value": obs_value, "obs_rinv": obs_rinv, "radius": radius}


highest = lax.Precision.HIGHEST

def block_points(band_id, tile_id, rows_dev):
    half_block = (BLOCK - 1) // 2
    row_blocks = rows_dev // BLOCK
    col_blocks = COLS // BLOCK
    row_ids = band_id * rows_dev + BLOCK * jnp.arange(row_blocks, dtype=jnp.int32) + half_block
    col_ids = tile_id * COLS + BLOCK * jnp.arange(col_blocks, dtype=jnp.int32) + half_block
    point_rows = jnp.broadcast_to(row_ids[:, None], (row_blocks, col_blocks)).reshape(-1).astype(jnp.float32)
    point_cols = jnp.broadcast_to(col_ids[None, :], (row_blocks, col_blocks)).reshape(-1).astype(jnp.float32)
    return (point_rows, point_cols)

def locality(obs_meta, point_rows, point_cols, extent, circle):
    row_gap = jnp.abs(obs_meta[2][None, :] - point_rows[:, None])
    col_gap = jnp.abs(obs_meta[3][None, :] - point_cols[:, None])
    col_gap = jnp.minimum(col_gap, circle - col_gap)
    taper = jnp.maximum(0.0, 1.0 - row_gap / extent) * jnp.maximum(0.0, 1.0 - col_gap / extent)
    return taper * obs_meta[1][None, :]

def accumulate(totals, ens_blk, meta_blk, point_rows, point_cols, extent, circle):
    gram_sum, rhs_sum = totals
    centre = lax.optimization_barrier(jnp.mean(ens_blk, axis=0))
    spread_obs = ens_blk - centre[None, :]
    innovation = meta_blk[0] - centre
    weights = locality(meta_blk, point_rows, point_cols, extent, circle)
    weighted = weights[:, None, :] * spread_obs[None, :, :]
    gram_sum = gram_sum + jnp.einsum('pkj,lj->pkl', weighted, spread_obs, precision=highest)
    rhs_sum = rhs_sum + jnp.einsum('pkj,j->pk', weighted, innovation, precision=highest)
    return (gram_sum, rhs_sum)

def transform(gram_sum, rhs_sum, members):
    identity = jnp.eye(members, dtype=gram_sum.dtype)
    gram_full = gram_sum + (members - 1.0) * identity[None]
    frob_norm = jnp.sqrt(lax.optimization_barrier(jnp.sum(gram_full * gram_full, axis=(1, 2))))
    iterate = gram_full / frob_norm[:, None, None]
    inv_root = jnp.broadcast_to(identity, gram_full.shape)
    for sweep in range(NS_ITERS):
        middle = 1.5 * identity[None] - 0.5 * jnp.einsum('pij,pjk->pik', inv_root, iterate, precision=highest)
        iterate = jnp.einsum('pij,pjk->pik', iterate, middle, precision=highest)
        inv_root = jnp.einsum('pij,pjk->pik', middle, inv_root, precision=highest)
    inv_root = inv_root / jnp.sqrt(frob_norm)[:, None, None]
    inner = jnp.einsum('pij,pj->pi', inv_root, rhs_sum, precision=highest)
    mean_shift = jnp.einsum('pij,pj->pi', inv_root, inner, precision=highest)
    return jnp.sqrt(members - 1.0) * inv_root + mean_shift[:, :, None]

def apply_mix(band_state, mixing, rows_dev):
    members = band_state.shape[0]
    row_blocks = rows_dev // BLOCK
    col_blocks = COLS // BLOCK
    cell_grid = band_state.reshape(members, row_blocks, BLOCK, col_blocks, BLOCK)
    centre = lax.optimization_barrier(jnp.mean(cell_grid, axis=0))
    spread_state = cell_grid - centre[None]
    mix_blocks = mixing.reshape(row_blocks, col_blocks, members, members)
    result = jnp.einsum('ablk,laibj->kaibj', mix_blocks, spread_state, precision=highest) + centre[None]
    return result.reshape(members, rows_dev * COLS)

def reference(state, obs_index, obs_count, obs_value, obs_rinv, radius):
    members = state.shape[0]
    tile_count = state.shape[1]
    cell_count = state.shape[2]
    rows_dev = LAT // N_MEM
    band_cells = rows_dev * COLS
    circle = 1.0 * COLS * tile_count
    ens_obs = jax.vmap(lambda field_rows, cell_ids: field_rows[:, cell_ids], in_axes=(1, 0), out_axes=1)(state, obs_index)
    slot_ids = jnp.arange(SLOTS, dtype=jnp.int32)
    is_live = slot_ids[None, :] < obs_count[:, None]
    rinv_live = jnp.where(is_live, obs_rinv, 0.0)
    tile_ids = jnp.arange(tile_count, dtype=jnp.int32)
    obs_row = (obs_index // COLS).astype(jnp.float32)
    obs_col = (obs_index % COLS + tile_ids[:, None] * COLS).astype(jnp.float32)
    obs_meta = jnp.stack([obs_value, rinv_live, obs_row, obs_col])
    stacked = jnp.concatenate([ens_obs, obs_meta], axis=0)
    offsets = jnp.arange(-HALO, HALO + 1, dtype=jnp.int32)

    def per_tile(tile_id):
        window = stacked[:, (tile_id + offsets) % tile_count, :].reshape(members + 4, -1)
        ens_win = window[:members]
        meta_win = window[members:]
        extent = (radius[tile_id] * COLS).astype(jnp.float32)
        tile_state = lax.dynamic_index_in_dim(state, tile_id, axis=1, keepdims=False)
        band_rows = tile_state.reshape(members, N_MEM, band_cells).transpose(1, 0, 2)

        def per_band(pair_item):
            band_id, band_state = pair_item
            point_rows, point_cols = block_points(band_id, tile_id, rows_dev)
            points = point_rows.shape[0]
            totals = (jnp.zeros((points, members, members), jnp.float32), jnp.zeros((points, members), jnp.float32))
            gram_sum, rhs_sum = accumulate(totals, ens_win, meta_win, point_rows, point_cols, extent, circle)
            mixing = transform(gram_sum, rhs_sum, members)
            return apply_mix(band_state, mixing, rows_dev)
        result = lax.map(per_band, (jnp.arange(N_MEM, dtype=jnp.int32), band_rows))
        return result.transpose(1, 0, 2).reshape(members, cell_count)
    outcome = lax.map(per_tile, tile_ids)
    return outcome.transpose(1, 0, 2)
```

```python
import functools
import math

import jax
import jax.numpy as jnp
import numpy as np
from jax import lax
from jax.experimental import pallas as pl
from jax.experimental.pallas import tpu as pltpu
from jax.sharding import PartitionSpec as P

COLS = 45
BLOCK = 9
HALO = 2
NS_ITERS = 4
LANES = 128
MESH = pl.DeviceIdType.MESH


def ceil_to(x, m):
    return (x + m - 1) // m * m


def split(x, parts):
    out = []
    for _ in range(parts):
        piece = x.astype(jnp.bfloat16)
        out.append(piece)
        x = x - piece.astype(jnp.float32)
    return out


def dot(a, b):
    return jnp.dot(a, b, preferred_element_type=jnp.float32)


def dot_nt(a, b):
    return lax.dot_general(a, b, (((1,), (1,)), ((), ())), preferred_element_type=jnp.float32)


def iota(shape, dim):
    return lax.broadcasted_iota(jnp.int32, shape, dim)


def kernel(
    dims,
    count_ref, radius_ref, state_ref, index_ref, value_ref, rinv_ref, block_ref,
    out_ref,
    own_ref, obs_ref, recv_ref, back_ref, pert_ref, prs_ref, gram_ref, y_ref, z_ref, m_ref, t_ref,
    vec_ref, obs_send, obs_recv, st_send, st_recv, bk_send, bk_recv,
):
    groups, tiles, mem_dev, slots, band_cells, width, points = dims
    members = groups * mem_dev
    mpad = gram_ref.shape[1]
    rows_dev = band_cells // COLS
    col_blocks = COLS // BLOCK
    me = lax.axis_index("mem")
    tile = lax.axis_index("tile")
    offsets = list(range(-HALO, HALO + 1))
    peers = [(s, d) for d in offsets for s in range(groups) if (s, d) != (0, 0)]

    def member(s):
        return lax.rem(me + s, groups)

    def column(d):
        return lax.rem(tile + d + tiles, tiles)

    barrier = pltpu.get_barrier_semaphore()
    for s, d in peers:
        pl.semaphore_signal(barrier, inc=1, device_id=(member(s), column(d)), device_id_type=MESH)

    cell = index_ref[...]
    cell_f = cell.astype(jnp.float32)
    band = jnp.floor((cell_f + 0.5) * (1.0 / band_cells))
    inside = cell_f - band * band_cells
    strip = jnp.floor((inside + 0.5) * (1.0 / LANES))
    lane = inside - strip * LANES
    strips = width // LANES
    row_id = (band * strips + strip).astype(jnp.int32)
    lane_id = lane.astype(jnp.int32)
    lane_hot = jnp.where(iota((LANES, slots), 0) == lane_id, 1.0, 0.0).astype(jnp.bfloat16)
    dev_pad = ceil_to(mem_dev, 8)
    pieces = []
    for b in range(groups):
        rows = state_ref[b]
        if dev_pad > mem_dev:
            rows = jnp.concatenate([rows, jnp.zeros((dev_pad - mem_dev, width), jnp.float32)], axis=0)
        for r in range(strips):
            pieces.append(rows[:, r * LANES : (r + 1) * LANES])
    table = jnp.concatenate(pieces, axis=0)
    picked = sum(dot(part, lane_hot) for part in split(table, 3))
    own = jnp.zeros((dev_pad, slots), jnp.float32)
    for r in range(groups * strips):
        own = own + jnp.where(row_id == r, picked[r * dev_pad : (r + 1) * dev_pad], 0.0)
    live = jnp.where(iota((1, slots), 1) < count_ref[0], rinv_ref[...], 0.0)
    payload = jnp.concatenate([own[:mem_dev], value_ref[...], live, cell_f], axis=0)
    own_ref[...] = payload
    obs_ref[me, HALO] = payload
    recv_ref[me] = state_ref[me]

    pl.semaphore_wait(barrier, len(peers))

    def obs_copy(n, s, d):
        return pltpu.make_async_remote_copy(
            src_ref=own_ref,
            dst_ref=obs_ref.at[me, HALO - d],
            send_sem=obs_send.at[n],
            recv_sem=obs_recv.at[me, HALO - d],
            device_id=(member(s), column(d)),
            device_id_type=MESH,
        )

    def obs_wait(n, s, d):
        src = member(s)
        return pltpu.make_async_remote_copy(
            src_ref=own_ref,
            dst_ref=obs_ref.at[src, HALO + d],
            send_sem=obs_send.at[n],
            recv_sem=obs_recv.at[src, HALO + d],
            device_id=(src, column(d)),
            device_id_type=MESH,
        )

    def band_copy(s, src_ref, dst_ref, send, recv):
        to = member(s)
        return pltpu.make_async_remote_copy(
            src_ref=src_ref.at[to], dst_ref=dst_ref.at[me], send_sem=send.at[s],
            recv_sem=recv.at[me], device_id=(to, tile), device_id_type=MESH,
        )

    def band_wait(s, src_ref, dst_ref, send, recv):
        to = member(s)
        return pltpu.make_async_remote_copy(
            src_ref=src_ref.at[to], dst_ref=dst_ref.at[to], send_sem=send.at[s],
            recv_sem=recv.at[to], device_id=(to, tile), device_id_type=MESH,
        )

    for n, (s, d) in enumerate(peers):
        obs_copy(n, s, d).start()
    for s in range(1, groups):
        band_copy(s, state_ref, recv_ref, st_send, st_recv).start()
    for n, (s, d) in enumerate(peers):
        obs_wait(n, s, d).wait_recv()

    point = iota((points, 1), 0).astype(jnp.float32)
    point_row = jnp.floor((point + 0.5) * (1.0 / col_blocks))
    point_col = point - point_row * col_blocks
    half = (BLOCK - 1) // 2
    prow = point_row * BLOCK + (me * rows_dev + half).astype(jnp.float32)
    pcol = point_col * BLOCK + (tile * COLS + half).astype(jnp.float32)
    extent = jnp.full((1, 1), radius_ref[0] * COLS, jnp.int32).astype(jnp.float32)
    circle = float(COLS * tiles)
    weights = []
    for at, d in enumerate(offsets):
        ens = jnp.concatenate([obs_ref[g, at][:mem_dev] for g in range(groups)], axis=0)
        meta = obs_ref[0, at]
        centre = jnp.sum(ens, axis=0, keepdims=True) * (1.0 / members)
        innovation = meta[mem_dev : mem_dev + 1] - centre
        parts = [ens - centre, innovation]
        if mpad > members + 1:
            parts.append(jnp.zeros((mpad - members - 1, slots), jnp.float32))
        pert_ref[:, at * slots : (at + 1) * slots] = jnp.concatenate(parts, axis=0)
        where = meta[mem_dev + 2 : mem_dev + 3]
        obs_row = jnp.floor((where + 0.5) * (1.0 / COLS))
        obs_col = where - obs_row * COLS + (column(d) * COLS).astype(jnp.float32)
        rgap = jnp.abs(obs_row - prow)
        cgap = jnp.abs(obs_col - pcol)
        cgap = jnp.minimum(cgap, circle - cgap)
        taper = jnp.maximum(0.0, 1.0 - rgap / extent) * jnp.maximum(0.0, 1.0 - cgap / extent)
        weights.append(taper * meta[mem_dev + 1 : mem_dev + 2])
    w_hi, w_lo = split(jnp.concatenate(weights, axis=1), 2)

    batch = prs_ref.shape[0] // mpad

    def gram_group(i, _):
        for k in range(batch):
            prs_ref[k * mpad : (k + 1) * mpad] = pert_ref[pl.ds(i * batch + k, 1)] * pert_ref[...]
        p_hi, p_lo = split(prs_ref[...], 2)
        total = dot_nt(p_hi, w_hi) + dot_nt(p_hi, w_lo) + dot_nt(p_lo, w_hi)
        for k in range(batch):
            gram_ref[i * batch + k] = total[k * mpad : (k + 1) * mpad]
        return 0

    if batch == members:
        gram_group(0, 0)
    else:
        lax.fori_loop(0, members // batch, gram_group, 0)

    full = (members, mpad, points)
    eye = jnp.where(iota((members, mpad, 1), 0) == iota((members, mpad, 1), 1), 1.0, 0.0)
    inside_rows = iota((1, mpad, 1), 1) < members
    g = jnp.where(inside_rows, gram_ref[...], 0.0) + (members - 1.0) * eye
    frob = jnp.sqrt(jnp.sum(jnp.sum(g * g, axis=0), axis=0, keepdims=True))
    y_ref[...] = g / frob[None]
    z_ref[...] = 1.5 * eye - 0.5 * y_ref[...]

    step = 4 if members % 4 == 0 else 1

    def product(a_ref, b_ref, o_ref, finish):
        def body(i, _):
            rows = [i * step + u for u in range(step)]
            acc = [None] * step
            for k in range(members):
                right = b_ref[k]
                for u in range(step):
                    term = a_ref[rows[u], k : k + 1, :] * right
                    acc[u] = term if acc[u] is None else acc[u] + term
            for u in range(step):
                o_ref[rows[u]] = finish(rows[u], acc[u])
            return 0

        lax.fori_loop(0, members // step, body, 0)

    def keep(_, x):
        return x

    def middle(i, x):
        return jnp.where(iota((mpad, 1), 0) == i, 1.5, 0.0) - 0.5 * x

    product(y_ref, z_ref, t_ref, keep)
    y, y_other, z, z_other = t_ref, y_ref, z_ref, None
    spare = [y_other]
    for sweep in range(1, NS_ITERS):
        product(z, y, m_ref, middle)
        if sweep < NS_ITERS - 1:
            new_y = spare.pop()
            product(y, m_ref, new_y, keep)
            old_y = y
            product(m_ref, z, old_y, keep)
            spare.append(z)
            y, z = new_y, old_y
        else:
            new_z = spare.pop()
            product(m_ref, z, new_z, keep)
            z = new_z
    root = z[...] * (1.0 / jnp.sqrt(frob))[None]
    z[...] = root
    inner = sum(z[k] * gram_ref[k, members : members + 1, :] for k in range(members))
    vec_ref[...] = inner
    shift = sum(z[k] * vec_ref[k : k + 1, :] for k in range(members))
    vec_ref[...] = shift
    scale = math.sqrt(members - 1.0)
    for l in range(members):
        z[l] = scale * z[l] + vec_ref[l : l + 1, :]

    for s in range(1, groups):
        band_wait(s, state_ref, recv_ref, st_send, st_recv).wait_recv()
    chunk = 2 * LANES if width % (2 * LANES) == 0 else LANES

    def mix_chunk(c, _):
        span = pl.ds(pl.multiple_of(c * chunk, chunk), chunk)
        hot = jnp.where(iota((points, chunk), 0) == block_ref[:, span], 1.0, 0.0).astype(jnp.bfloat16)
        total = jnp.zeros((1, chunk), jnp.float32)
        for g in range(groups):
            total = total + jnp.sum(recv_ref[g, :, span], axis=0, keepdims=True)
        mean = total * (1.0 / members)
        acc = jnp.broadcast_to(mean, (mpad, chunk))
        for l0 in range(0, members, batch):
            mix = z[l0 : l0 + batch].reshape(batch * mpad, points)
            spread = sum(dot(part, hot) for part in split(mix, 2))
            for l in range(batch):
                q, r = divmod(l0 + l, mem_dev)
                dev = recv_ref[q, r : r + 1, span] - mean
                acc = acc + spread[l * mpad : (l + 1) * mpad] * dev
        for g in range(groups):
            back_ref[g, :, span] = acc[g * mem_dev : (g + 1) * mem_dev]
        return 0

    lax.fori_loop(0, width // chunk, mix_chunk, 0)
    for s in range(1, groups):
        band_copy(s, back_ref, out_ref, bk_send, bk_recv).start()
    out_ref[me] = back_ref[me]
    for n, (s, d) in enumerate(peers):
        obs_copy(n, s, d).wait_send()
    for s in range(1, groups):
        band_copy(s, state_ref, recv_ref, st_send, st_recv).wait_send()
    for s in range(1, groups):
        band_wait(s, back_ref, out_ref, bk_send, bk_recv).wait()


def shards(groups, tiles, state, obs_index, obs_count, obs_value, obs_rinv, radius):
    mem_dev, _, cells = state.shape
    slots = obs_index.shape[1]
    members = groups * mem_dev
    band_cells = cells // groups
    width = ceil_to(band_cells, LANES)
    points = (band_cells // COLS // BLOCK) * (COLS // BLOCK)
    mpad = ceil_to(members + 1, 8)
    window = (2 * HALO + 1) * slots
    batch = max(b for b in range(1, members + 1) if members % b == 0 and (b == 1 or b * mpad <= 512))
    bands = state.reshape(mem_dev, groups, band_cells).transpose(1, 0, 2)
    bands = jnp.pad(bands, ((0, 0), (0, 0), (0, width - band_cells)))
    at = np.arange(width)
    block_of = (at // COLS // BLOCK) * (COLS // BLOCK) + at % COLS // BLOCK
    block_of = jnp.asarray(block_of[None].astype(np.int32))
    dims = (groups, tiles, mem_dev, slots, band_cells, width, points)
    peers = groups * (2 * HALO + 1) - 1
    f32 = jnp.float32
    vmem = pl.BlockSpec(memory_space=pltpu.VMEM)
    smem = pl.BlockSpec(memory_space=pltpu.SMEM)
    banded = (groups, mem_dev, width)
    square = pltpu.VMEM((members, mpad, points), f32)
    dma = pltpu.SemaphoreType.DMA
    out = pl.pallas_call(
        functools.partial(kernel, dims),
        out_shape=jax.ShapeDtypeStruct(banded, f32),
        in_specs=[smem, smem] + [vmem] * 5,
        out_specs=vmem,
        scratch_shapes=[
            pltpu.VMEM((mem_dev + 3, slots), f32),
            pltpu.VMEM((groups, 2 * HALO + 1, mem_dev + 3, slots), f32),
            pltpu.VMEM(banded, f32),
            pltpu.VMEM(banded, f32),
            pltpu.VMEM((mpad, window), f32),
            pltpu.VMEM((batch * mpad, window), f32),
            square, square, square, square, square,
            pltpu.VMEM((mpad, points), f32),
            dma((peers,)),
            dma((groups, 2 * HALO + 1)),
            dma((groups,)), dma((groups,)), dma((groups,)), dma((groups,)),
        ],
        compiler_params=pltpu.CompilerParams(collective_id=0, has_side_effects=True),
    )(obs_count, radius, bands, obs_index, obs_value, obs_rinv, block_of)
    out = out[:, :, :band_cells].transpose(1, 0, 2)
    return out.reshape(mem_dev, 1, cells)


def solution(mesh):
    in_specs = (
        P("mem", "tile", None),
        P("tile", None),
        P("tile"),
        P("tile", None),
        P("tile", None),
        P("tile"),
    )
    return jax.shard_map(
        functools.partial(shards, mesh.shape["mem"], mesh.shape["tile"]),
        mesh=mesh, in_specs=in_specs, out_specs=P("mem", "tile", None), check_vma=False,
    )
```

```python
import functools
import math

import jax
import jax.numpy as jnp
import numpy as np
from jax import lax
from jax.experimental import pallas as pl
from jax.experimental.pallas import tpu as pltpu
from jax.sharding import PartitionSpec as P

COLS = 45
BLOCK = 9
HALO = 2
NS_ITERS = 4
LANES = 128
SEGMENTS = 4
MESH = pl.DeviceIdType.MESH


def ceil_to(x, m):
    return (x + m - 1) // m * m


def split(x, parts):
    out = []
    for _ in range(parts):
        piece = x.astype(jnp.bfloat16)
        out.append(piece)
        x = x - piece.astype(jnp.float32)
    return out


def dot(a, b):
    return jnp.dot(a, b, preferred_element_type=jnp.float32)


def dot_nt(a, b):
    return lax.dot_general(a, b, (((1,), (1,)), ((), ())), preferred_element_type=jnp.float32)


def iota(shape, dim):
    return lax.broadcasted_iota(jnp.int32, shape, dim)


def kernel(
    dims,
    count_ref, radius_ref, state_ref, index_ref, value_ref, rinv_ref, block_ref,
    out_ref,
    own_ref, own_meta_ref, obs_ref, meta_ref, recv_ref, back_ref, pert_ref, prs_ref, gram_ref, y_ref, z_ref, m_ref, t_ref,
    vec_ref, obs_send, obs_recv, meta_send, meta_recv, st_send, st_recv, bk_send, bk_recv,
):
    groups, tiles, mem_dev, slots, band_cells, width, points = dims
    members = groups * mem_dev
    mpad = gram_ref.shape[1]
    rows_dev = band_cells // COLS
    col_blocks = COLS // BLOCK
    me = lax.axis_index("mem")
    tile = lax.axis_index("tile")
    offsets = list(range(-HALO, HALO + 1))
    peers = [(s, d) for d in offsets for s in range(groups) if (s, d) != (0, 0)]

    def member(s):
        return lax.rem(me + s, groups)

    def column(d):
        return lax.rem(tile + d + tiles, tiles)

    barrier = pltpu.get_barrier_semaphore()
    for s, d in peers:
        pl.semaphore_signal(barrier, inc=1, device_id=(member(s), column(d)), device_id_type=MESH)

    cell = index_ref[...]
    cell_f = cell.astype(jnp.float32)
    band = jnp.floor((cell_f + 0.5) * (1.0 / band_cells))
    inside = cell_f - band * band_cells
    strip = jnp.floor((inside + 0.5) * (1.0 / LANES))
    lane = inside - strip * LANES
    strips = width // LANES
    row_id = (band * strips + strip).astype(jnp.int32)
    lane_id = lane.astype(jnp.int32)
    lane_hot = jnp.where(iota((LANES, slots), 0) == lane_id, 1.0, 0.0).astype(jnp.bfloat16)
    dev_pad = ceil_to(mem_dev, 8)
    pieces = []
    for b in range(groups):
        rows = state_ref[b]
        if dev_pad > mem_dev:
            rows = jnp.concatenate([rows, jnp.zeros((dev_pad - mem_dev, width), jnp.float32)], axis=0)
        for r in range(strips):
            pieces.append(rows[:, r * LANES : (r + 1) * LANES])
    table = jnp.concatenate(pieces, axis=0)
    picked = sum(dot(part, lane_hot) for part in split(table, 3))
    own = jnp.zeros((dev_pad, slots), jnp.float32)
    for r in range(groups * strips):
        own = own + jnp.where(row_id == r, picked[r * dev_pad : (r + 1) * dev_pad], 0.0)
    live = jnp.where(iota((1, slots), 1) < count_ref[0], rinv_ref[...], 0.0)
    own_ref[...] = own[:mem_dev]
    obs_ref[me, HALO] = own[:mem_dev]
    about = jnp.concatenate([value_ref[...], live, cell_f], axis=0)
    own_meta_ref[...] = about
    meta_ref[HALO] = about
    recv_ref[me] = state_ref[me]

    pl.semaphore_wait(barrier, len(peers))

    def obs_copy(n, s, d):
        return pltpu.make_async_remote_copy(
            src_ref=own_ref,
            dst_ref=obs_ref.at[me, HALO - d],
            send_sem=obs_send.at[n],
            recv_sem=obs_recv.at[me, HALO - d],
            device_id=(member(s), column(d)),
            device_id_type=MESH,
        )

    def obs_wait(n, s, d):
        src = member(s)
        return pltpu.make_async_remote_copy(
            src_ref=own_ref,
            dst_ref=obs_ref.at[src, HALO + d],
            send_sem=obs_send.at[n],
            recv_sem=obs_recv.at[src, HALO + d],
            device_id=(src, column(d)),
            device_id_type=MESH,
        )

    def meta_copy(d, slot, from_tile):
        return pltpu.make_async_remote_copy(
            src_ref=own_meta_ref, dst_ref=meta_ref.at[slot], send_sem=meta_send.at[HALO + d],
            recv_sem=meta_recv.at[slot], device_id=(me, from_tile), device_id_type=MESH,
        )

    chunk = 2 * LANES if width % (2 * LANES) == 0 else LANES
    chunks = width // chunk
    bounds = [chunks * i // SEGMENTS for i in range(SEGMENTS + 1)]
    segments = [(a, b) for a, b in zip(bounds, bounds[1:]) if b > a]

    def lanes_of(i):
        a, b = segments[i]
        return pl.ds(a * chunk, (b - a) * chunk)

    def band_copy(s, i, src_ref, dst_ref, send, recv):
        to = member(s)
        return pltpu.make_async_remote_copy(
            src_ref=src_ref.at[to, :, lanes_of(i)], dst_ref=dst_ref.at[me, :, lanes_of(i)],
            send_sem=send.at[s, i], recv_sem=recv.at[me, i],
            device_id=(to, tile), device_id_type=MESH,
        )

    def band_wait(s, i, src_ref, dst_ref, send, recv):
        to = member(s)
        return pltpu.make_async_remote_copy(
            src_ref=src_ref.at[to, :, lanes_of(i)], dst_ref=dst_ref.at[to, :, lanes_of(i)],
            send_sem=send.at[s, i], recv_sem=recv.at[to, i],
            device_id=(to, tile), device_id_type=MESH,
        )

    near = [d for d in offsets if d != 0]
    for d in near:
        meta_copy(d, HALO - d, column(d)).start()

    for n, (s, d) in enumerate(peers):
        obs_copy(n, s, d).start()
    for i in range(len(segments)):
        for s in range(1, groups):
            band_copy(s, i, state_ref, recv_ref, st_send, st_recv).start()
    for d in near:
        meta_copy(d, HALO + d, column(d)).wait_recv()
    for n, (s, d) in enumerate(peers):
        obs_wait(n, s, d).wait_recv()

    point = iota((points, 1), 0).astype(jnp.float32)
    point_row = jnp.floor((point + 0.5) * (1.0 / col_blocks))
    point_col = point - point_row * col_blocks
    half = (BLOCK - 1) // 2
    prow = point_row * BLOCK + (me * rows_dev + half).astype(jnp.float32)
    pcol = point_col * BLOCK + (tile * COLS + half).astype(jnp.float32)
    extent = jnp.full((1, 1), radius_ref[0] * COLS, jnp.int32).astype(jnp.float32)
    circle = float(COLS * tiles)
    weights = []
    for at, d in enumerate(offsets):
        ens = jnp.concatenate([obs_ref[g, at] for g in range(groups)], axis=0)
        meta = meta_ref[at]
        centre = jnp.sum(ens, axis=0, keepdims=True) * (1.0 / members)
        innovation = meta[0:1] - centre
        parts = [ens - centre, innovation]
        if mpad > members + 1:
            parts.append(jnp.zeros((mpad - members - 1, slots), jnp.float32))
        pert_ref[:, at * slots : (at + 1) * slots] = jnp.concatenate(parts, axis=0)
        where = meta[2:3]
        obs_row = jnp.floor((where + 0.5) * (1.0 / COLS))
        obs_col = where - obs_row * COLS + (column(d) * COLS).astype(jnp.float32)
        rgap = jnp.abs(obs_row - prow)
        cgap = jnp.abs(obs_col - pcol)
        cgap = jnp.minimum(cgap, circle - cgap)
        taper = jnp.maximum(0.0, 1.0 - rgap / extent) * jnp.maximum(0.0, 1.0 - cgap / extent)
        weights.append(taper * meta[1:2])
    w_hi, w_lo = split(jnp.concatenate(weights, axis=1), 2)

    batch = prs_ref.shape[0] // mpad

    def gram_group(i, _):
        for k in range(batch):
            prs_ref[k * mpad : (k + 1) * mpad] = pert_ref[pl.ds(i * batch + k, 1)] * pert_ref[...]
        p_hi, p_lo = split(prs_ref[...], 2)
        total = dot_nt(p_hi, w_hi) + dot_nt(p_hi, w_lo) + dot_nt(p_lo, w_hi)
        for k in range(batch):
            gram_ref[i * batch + k] = total[k * mpad : (k + 1) * mpad]
        return 0

    if batch == members:
        gram_group(0, 0)
    else:
        lax.fori_loop(0, members // batch, gram_group, 0)

    full = (members, mpad, points)
    eye = jnp.where(iota((members, mpad, 1), 0) == iota((members, mpad, 1), 1), 1.0, 0.0)
    inside_rows = iota((1, mpad, 1), 1) < members
    g = jnp.where(inside_rows, gram_ref[...], 0.0) + (members - 1.0) * eye
    frob = jnp.sqrt(jnp.sum(jnp.sum(g * g, axis=0), axis=0, keepdims=True))
    y_ref[...] = g / frob[None]
    z_ref[...] = 1.5 * eye - 0.5 * y_ref[...]

    step = 4 if members % 4 == 0 else 1

    def product(a_ref, b_ref, o_ref, finish):
        def body(i, _):
            rows = [i * step + u for u in range(step)]
            acc = [None] * step
            for k in range(members):
                right = b_ref[k]
                for u in range(step):
                    term = a_ref[rows[u], k : k + 1, :] * right
                    acc[u] = term if acc[u] is None else acc[u] + term
            for u in range(step):
                o_ref[rows[u]] = finish(rows[u], acc[u])
            return 0

        lax.fori_loop(0, members // step, body, 0)

    def keep(_, x):
        return x

    def middle(i, x):
        return jnp.where(iota((mpad, 1), 0) == i, 1.5, 0.0) - 0.5 * x

    product(y_ref, z_ref, t_ref, keep)
    y, y_other, z, z_other = t_ref, y_ref, z_ref, None
    spare = [y_other]
    for sweep in range(1, NS_ITERS):
        product(z, y, m_ref, middle)
        if sweep < NS_ITERS - 1:
            new_y = spare.pop()
            product(y, m_ref, new_y, keep)
            old_y = y
            product(m_ref, z, old_y, keep)
            spare.append(z)
            y, z = new_y, old_y
        else:
            new_z = spare.pop()
            product(m_ref, z, new_z, keep)
            z = new_z
    root = z[...] * (1.0 / jnp.sqrt(frob))[None]
    z[...] = root
    inner = sum(z[k] * gram_ref[k, members : members + 1, :] for k in range(members))
    vec_ref[...] = inner
    shift = sum(z[k] * vec_ref[k : k + 1, :] for k in range(members))
    vec_ref[...] = shift
    scale = math.sqrt(members - 1.0)
    for l in range(members):
        z[l] = scale * z[l] + vec_ref[l : l + 1, :]

    def mix_chunk(c, _):
        span = pl.ds(pl.multiple_of(c * chunk, chunk), chunk)
        hot = jnp.where(iota((points, chunk), 0) == block_ref[:, span], 1.0, 0.0).astype(jnp.bfloat16)
        total = jnp.zeros((1, chunk), jnp.float32)
        for g in range(groups):
            total = total + jnp.sum(recv_ref[g, :, span], axis=0, keepdims=True)
        mean = total * (1.0 / members)
        acc = jnp.broadcast_to(mean, (mpad, chunk))
        for l0 in range(0, members, batch):
            mix = z[l0 : l0 + batch].reshape(batch * mpad, points)
            spread = sum(dot(part, hot) for part in split(mix, 2))
            for l in range(batch):
                q, r = divmod(l0 + l, mem_dev)
                dev = recv_ref[q, r : r + 1, span] - mean
                acc = acc + spread[l * mpad : (l + 1) * mpad] * dev
        for g in range(groups):
            back_ref[g, :, span] = acc[g * mem_dev : (g + 1) * mem_dev]
        return 0

    for i, (first, last) in enumerate(segments):
        for s in range(1, groups):
            band_wait(s, i, state_ref, recv_ref, st_send, st_recv).wait_recv()
        lax.fori_loop(first, last, mix_chunk, 0)
        for s in range(1, groups):
            band_copy(s, i, back_ref, out_ref, bk_send, bk_recv).start()
    out_ref[me] = back_ref[me]
    for n, (s, d) in enumerate(peers):
        obs_copy(n, s, d).wait_send()
    for d in near:
        meta_copy(d, HALO - d, column(d)).wait_send()
    for i in range(len(segments)):
        for s in range(1, groups):
            band_copy(s, i, state_ref, recv_ref, st_send, st_recv).wait_send()
    for i in range(len(segments)):
        for s in range(1, groups):
            band_wait(s, i, back_ref, out_ref, bk_send, bk_recv).wait()


def shards(groups, tiles, state, obs_index, obs_count, obs_value, obs_rinv, radius):
    mem_dev, _, cells = state.shape
    slots = obs_index.shape[1]
    members = groups * mem_dev
    band_cells = cells // groups
    width = ceil_to(band_cells, LANES)
    points = (band_cells // COLS // BLOCK) * (COLS // BLOCK)
    mpad = ceil_to(members + 1, 8)
    window = (2 * HALO + 1) * slots
    batch = max(b for b in range(1, members + 1) if members % b == 0 and (b == 1 or b * mpad <= 512))
    bands = state.reshape(mem_dev, groups, band_cells).transpose(1, 0, 2)
    bands = jnp.pad(bands, ((0, 0), (0, 0), (0, width - band_cells)))
    at = np.arange(width)
    block_of = (at // COLS // BLOCK) * (COLS // BLOCK) + at % COLS // BLOCK
    block_of = jnp.asarray(block_of[None].astype(np.int32))
    dims = (groups, tiles, mem_dev, slots, band_cells, width, points)
    peers = groups * (2 * HALO + 1) - 1
    f32 = jnp.float32
    vmem = pl.BlockSpec(memory_space=pltpu.VMEM)
    smem = pl.BlockSpec(memory_space=pltpu.SMEM)
    banded = (groups, mem_dev, width)
    square = pltpu.VMEM((members, mpad, points), f32)
    dma = pltpu.SemaphoreType.DMA
    out = pl.pallas_call(
        functools.partial(kernel, dims),
        out_shape=jax.ShapeDtypeStruct(banded, f32),
        in_specs=[smem, smem] + [vmem] * 5,
        out_specs=vmem,
        scratch_shapes=[
            pltpu.VMEM((mem_dev, slots), f32),
            pltpu.VMEM((3, slots), f32),
            pltpu.VMEM((groups, 2 * HALO + 1, mem_dev, slots), f32),
            pltpu.VMEM((2 * HALO + 1, 3, slots), f32),
            pltpu.VMEM(banded, f32),
            pltpu.VMEM(banded, f32),
            pltpu.VMEM((mpad, window), f32),
            pltpu.VMEM((batch * mpad, window), f32),
            square, square, square, square, square,
            pltpu.VMEM((mpad, points), f32),
            dma((peers,)),
            dma((groups, 2 * HALO + 1)),
            dma((2 * HALO + 1,)), dma((2 * HALO + 1,)),
            dma((groups, SEGMENTS)), dma((groups, SEGMENTS)),
            dma((groups, SEGMENTS)), dma((groups, SEGMENTS)),
        ],
        compiler_params=pltpu.CompilerParams(collective_id=0, has_side_effects=True),
    )(obs_count, radius, bands, obs_index, obs_value, obs_rinv, block_of)
    out = out[:, :, :band_cells].transpose(1, 0, 2)
    return out.reshape(mem_dev, 1, cells)


def solution(mesh):
    in_specs = (
        P("mem", "tile", None),
        P("tile", None),
        P("tile"),
        P("tile", None),
        P("tile", None),
        P("tile"),
    )
    return jax.shard_map(
        functools.partial(shards, mesh.shape["mem"], mesh.shape["tile"]),
        mesh=mesh, in_specs=in_specs, out_specs=P("mem", "tile", None), check_vma=False,
    )
```

```python
import functools
import math

import jax
import jax.numpy as jnp
import numpy as np
from jax import lax
from jax.experimental import pallas as pl
from jax.experimental.pallas import tpu as pltpu
from jax.sharding import PartitionSpec as P

COLS = 45
BLOCK = 9
HALO = 2
NS_ITERS = 4
LANES = 128
MESH = pl.DeviceIdType.MESH


def ceil_to(x, m):
    return (x + m - 1) // m * m


def split(x, parts):
    out = []
    for _ in range(parts):
        piece = x.astype(jnp.bfloat16)
        out.append(piece)
        x = x - piece.astype(jnp.float32)
    return out


def dot(a, b):
    return jnp.dot(a, b, preferred_element_type=jnp.float32)


def dot_nt(a, b):
    return lax.dot_general(a, b, (((1,), (1,)), ((), ())), preferred_element_type=jnp.float32)


def iota(shape, dim):
    return lax.broadcasted_iota(jnp.int32, shape, dim)


def kernel(
    dims,
    count_ref, radius_ref, state_ref, index_ref, value_ref, rinv_ref, block_ref,
    out_ref,
    own_ref, own_meta_ref, obs_ref, meta_ref, st_ref, recv_ref, back_ref, res_ref, pert_ref, prs_ref, gram_ref, y_ref, z_ref, m_ref, t_ref,
    vec_ref, obs_send, obs_recv, meta_send, meta_recv, st_send, st_recv, bk_send, bk_recv,
):
    groups, tiles, mem_dev, slots, band_cells, width, points = dims
    members = groups * mem_dev
    mpad = gram_ref.shape[1]
    rows_dev = band_cells // COLS
    col_blocks = COLS // BLOCK
    me = lax.axis_index("mem")
    tile = lax.axis_index("tile")
    offsets = list(range(-HALO, HALO + 1))
    peers = [(s, d) for d in offsets for s in range(groups) if (s, d) != (0, 0)]

    def member(s):
        return lax.rem(me + s, groups)

    def column(d):
        return lax.rem(tile + d + tiles, tiles)

    barrier = pltpu.get_barrier_semaphore()
    for s, d in peers:
        pl.semaphore_signal(barrier, inc=1, device_id=(member(s), column(d)), device_id_type=MESH)

    cell = index_ref[...]
    cell_f = cell.astype(jnp.float32)
    band = jnp.floor((cell_f + 0.5) * (1.0 / band_cells))
    inside = cell_f - band * band_cells
    strip = jnp.floor((inside + 0.5) * (1.0 / LANES))
    lane = inside - strip * LANES
    strips = width // LANES
    lane_hot = jnp.where(iota((LANES, slots), 0) == lane.astype(jnp.int32), 1.0, 0.0)
    lane_hot = lane_hot.astype(jnp.bfloat16)
    tall = st_ref.shape[1]
    row_strip = iota((tall, 1), 0) // mem_dev
    mine = jnp.where(iota((mem_dev, tall), 1) % mem_dev == iota((mem_dev, tall), 0), 1.0, 0.0)
    mine = mine.astype(jnp.bfloat16)
    own = jnp.zeros((mem_dev, slots), jnp.float32)
    for b in range(groups):
        rows = state_ref[b]
        for r in range(strips):
            st_ref[b, r * mem_dev : (r + 1) * mem_dev] = rows[:, r * LANES : (r + 1) * LANES]
        if tall > strips * mem_dev:
            st_ref[b, strips * mem_dev :] = jnp.zeros((tall - strips * mem_dev, LANES), jnp.float32)
    for b in range(groups):
        key = jnp.where(band == b, strip, -1.0).astype(jnp.int32)
        hit = row_strip == key
        for part in split(st_ref[b], 3):
            found = jnp.where(hit, dot(part, lane_hot), 0.0)
            own = own + dot(mine, found.astype(jnp.bfloat16))
    live = jnp.where(iota((1, slots), 1) < count_ref[0], rinv_ref[...], 0.0)
    own_ref[...] = own
    obs_ref[me, HALO] = own
    about = jnp.concatenate([value_ref[...], live, cell_f], axis=0)
    own_meta_ref[...] = about
    meta_ref[HALO] = about
    recv_ref[me] = st_ref[me]
    if tall > strips * mem_dev:
        pad = jnp.zeros((groups, tall - strips * mem_dev, LANES), jnp.float32)
        back_ref[:, strips * mem_dev :] = pad

    pl.semaphore_wait(barrier, len(peers))

    def obs_copy(n, s, d):
        return pltpu.make_async_remote_copy(
            src_ref=own_ref,
            dst_ref=obs_ref.at[me, HALO - d],
            send_sem=obs_send.at[n],
            recv_sem=obs_recv.at[me, HALO - d],
            device_id=(member(s), column(d)),
            device_id_type=MESH,
        )

    def obs_wait(n, s, d):
        src = member(s)
        return pltpu.make_async_remote_copy(
            src_ref=own_ref,
            dst_ref=obs_ref.at[src, HALO + d],
            send_sem=obs_send.at[n],
            recv_sem=obs_recv.at[src, HALO + d],
            device_id=(src, column(d)),
            device_id_type=MESH,
        )

    def meta_copy(d, slot, from_tile):
        return pltpu.make_async_remote_copy(
            src_ref=own_meta_ref, dst_ref=meta_ref.at[slot], send_sem=meta_send.at[HALO + d],
            recv_sem=meta_recv.at[slot], device_id=(me, from_tile), device_id_type=MESH,
        )

    per = 2 if strips % 2 == 0 else 1
    chunk = per * LANES
    segments = [(a, min(a + 8, strips)) for a in range(0, strips, 8)]

    def rows_of(i):
        a, b = segments[i]
        first = a * mem_dev
        return pl.ds(first, (tall if b == strips else b * mem_dev) - first)

    def band_copy(s, i, src_ref, dst_ref, send, recv):
        to = member(s)
        return pltpu.make_async_remote_copy(
            src_ref=src_ref.at[to, rows_of(i)], dst_ref=dst_ref.at[me, rows_of(i)],
            send_sem=send.at[s, i], recv_sem=recv.at[me, i],
            device_id=(to, tile), device_id_type=MESH,
        )

    def band_wait(s, i, src_ref, dst_ref, send, recv):
        to = member(s)
        return pltpu.make_async_remote_copy(
            src_ref=src_ref.at[to, rows_of(i)], dst_ref=dst_ref.at[to, rows_of(i)],
            send_sem=send.at[s, i], recv_sem=recv.at[to, i],
            device_id=(to, tile), device_id_type=MESH,
        )

    near = [d for d in offsets if d != 0]
    for d in near:
        meta_copy(d, HALO - d, column(d)).start()

    for n, (s, d) in enumerate(peers):
        obs_copy(n, s, d).start()
    for i in range(len(segments)):
        for s in range(1, groups):
            band_copy(s, i, st_ref, recv_ref, st_send, st_recv).start()
    for d in near:
        meta_copy(d, HALO + d, column(d)).wait_recv()
    for n, (s, d) in enumerate(peers):
        obs_wait(n, s, d).wait_recv()

    point = iota((points, 1), 0).astype(jnp.float32)
    point_row = jnp.floor((point + 0.5) * (1.0 / col_blocks))
    point_col = point - point_row * col_blocks
    half = (BLOCK - 1) // 2
    prow = point_row * BLOCK + (me * rows_dev + half).astype(jnp.float32)
    pcol = point_col * BLOCK + (tile * COLS + half).astype(jnp.float32)
    extent = jnp.full((1, 1), radius_ref[0] * COLS, jnp.int32).astype(jnp.float32)
    circle = float(COLS * tiles)
    weights = []
    for at, d in enumerate(offsets):
        ens = jnp.concatenate([obs_ref[g, at] for g in range(groups)], axis=0)
        meta = meta_ref[at]
        centre = jnp.sum(ens, axis=0, keepdims=True) * (1.0 / members)
        innovation = meta[0:1] - centre
        parts = [ens - centre, innovation]
        if mpad > members + 1:
            parts.append(jnp.zeros((mpad - members - 1, slots), jnp.float32))
        pert_ref[:, at * slots : (at + 1) * slots] = jnp.concatenate(parts, axis=0)
        where = meta[2:3]
        obs_row = jnp.floor((where + 0.5) * (1.0 / COLS))
        obs_col = where - obs_row * COLS + (column(d) * COLS).astype(jnp.float32)
        rgap = jnp.abs(obs_row - prow)
        cgap = jnp.abs(obs_col - pcol)
        cgap = jnp.minimum(cgap, circle - cgap)
        taper = jnp.maximum(0.0, 1.0 - rgap / extent) * jnp.maximum(0.0, 1.0 - cgap / extent)
        weights.append(taper * meta[1:2])
    w_hi, w_lo = split(jnp.concatenate(weights, axis=1), 2)

    batch = prs_ref.shape[0] // mpad

    def gram_group(i, _):
        for k in range(batch):
            prs_ref[k * mpad : (k + 1) * mpad] = pert_ref[pl.ds(i * batch + k, 1)] * pert_ref[...]
        p_hi, p_lo = split(prs_ref[...], 2)
        total = dot_nt(p_hi, w_hi) + dot_nt(p_hi, w_lo) + dot_nt(p_lo, w_hi)
        for k in range(batch):
            gram_ref[i * batch + k] = total[k * mpad : (k + 1) * mpad]
        return 0

    if batch == members:
        gram_group(0, 0)
    else:
        lax.fori_loop(0, members // batch, gram_group, 0)

    full = (members, mpad, points)
    eye = jnp.where(iota((members, mpad, 1), 0) == iota((members, mpad, 1), 1), 1.0, 0.0)
    inside_rows = iota((1, mpad, 1), 1) < members
    g = jnp.where(inside_rows, gram_ref[...], 0.0) + (members - 1.0) * eye
    frob = jnp.sqrt(jnp.sum(jnp.sum(g * g, axis=0), axis=0, keepdims=True))
    y_ref[...] = g / frob[None]
    z_ref[...] = 1.5 * eye - 0.5 * y_ref[...]

    step = 4 if members % 4 == 0 else 1

    def product(a_ref, b_ref, o_ref, finish):
        def body(i, _):
            rows = [i * step + u for u in range(step)]
            acc = [None] * step
            for k in range(members):
                right = b_ref[k]
                for u in range(step):
                    term = a_ref[rows[u], k : k + 1, :] * right
                    acc[u] = term if acc[u] is None else acc[u] + term
            for u in range(step):
                o_ref[rows[u]] = finish(rows[u], acc[u])
            return 0

        lax.fori_loop(0, members // step, body, 0)

    def keep(_, x):
        return x

    def middle(i, x):
        return jnp.where(iota((mpad, 1), 0) == i, 1.5, 0.0) - 0.5 * x

    product(y_ref, z_ref, t_ref, keep)
    y, y_other, z, z_other = t_ref, y_ref, z_ref, None
    spare = [y_other]
    for sweep in range(1, NS_ITERS):
        product(z, y, m_ref, middle)
        if sweep < NS_ITERS - 1:
            new_y = spare.pop()
            product(y, m_ref, new_y, keep)
            old_y = y
            product(m_ref, z, old_y, keep)
            spare.append(z)
            y, z = new_y, old_y
        else:
            new_z = spare.pop()
            product(m_ref, z, new_z, keep)
            z = new_z
    root = z[...] * (1.0 / jnp.sqrt(frob))[None]
    z[...] = root
    inner = sum(z[k] * gram_ref[k, members : members + 1, :] for k in range(members))
    vec_ref[...] = inner
    shift = sum(z[k] * vec_ref[k : k + 1, :] for k in range(members))
    vec_ref[...] = shift
    scale = math.sqrt(members - 1.0)
    for l in range(members):
        z[l] = scale * z[l] + vec_ref[l : l + 1, :]

    def mix_chunk(c, _):
        span = pl.ds(pl.multiple_of(c * chunk, chunk), chunk)
        hot = jnp.where(iota((points, chunk), 0) == block_ref[:, span], 1.0, 0.0).astype(jnp.bfloat16)

        def cells(l):
            q, r = divmod(l, mem_dev)
            rows = [recv_ref[q, pl.ds((c * per + j) * mem_dev + r, 1)] for j in range(per)]
            return jnp.concatenate(rows, axis=1)

        total = sum(cells(l) for l in range(members))
        mean = total * (1.0 / members)
        acc = jnp.broadcast_to(mean, (mpad, chunk))
        for l0 in range(0, members, batch):
            mix = z[l0 : l0 + batch].reshape(batch * mpad, points)
            spread = sum(dot(part, hot) for part in split(mix, 2))
            for l in range(batch):
                dev = cells(l0 + l) - mean
                acc = acc + spread[l * mpad : (l + 1) * mpad] * dev
        for g in range(groups):
            part = acc[g * mem_dev : (g + 1) * mem_dev]
            for j in range(per):
                back_ref[g, pl.ds((c * per + j) * mem_dev, mem_dev)] = part[:, j * LANES : (j + 1) * LANES]
        return 0

    for i, (first, last) in enumerate(segments):
        for s in range(1, groups):
            band_wait(s, i, st_ref, recv_ref, st_send, st_recv).wait_recv()
        lax.fori_loop(first // per, last // per, mix_chunk, 0)
        for s in range(1, groups):
            band_copy(s, i, back_ref, res_ref, bk_send, bk_recv).start()

    def deliver(g, src_ref, i):
        for r in range(*segments[i]):
            out_ref[g, :, r * LANES : (r + 1) * LANES] = src_ref[g, r * mem_dev : (r + 1) * mem_dev]

    for i in range(len(segments)):
        deliver(me, back_ref, i)
    for n, (s, d) in enumerate(peers):
        obs_copy(n, s, d).wait_send()
    for d in near:
        meta_copy(d, HALO - d, column(d)).wait_send()
    for i in range(len(segments)):
        for s in range(1, groups):
            band_copy(s, i, st_ref, recv_ref, st_send, st_recv).wait_send()
    for i in range(len(segments)):
        for s in range(1, groups):
            band_wait(s, i, back_ref, res_ref, bk_send, bk_recv).wait()
            deliver(member(s), res_ref, i)


def shards(groups, tiles, state, obs_index, obs_count, obs_value, obs_rinv, radius):
    mem_dev, _, cells = state.shape
    slots = obs_index.shape[1]
    members = groups * mem_dev
    band_cells = cells // groups
    width = ceil_to(band_cells, LANES)
    points = (band_cells // COLS // BLOCK) * (COLS // BLOCK)
    mpad = ceil_to(members + 1, 8)
    window = (2 * HALO + 1) * slots
    batch = max(b for b in range(1, members + 1) if members % b == 0 and (b == 1 or b * mpad <= 512))
    bands = state.reshape(mem_dev, groups, band_cells).transpose(1, 0, 2)
    bands = jnp.pad(bands, ((0, 0), (0, 0), (0, width - band_cells)))
    at = np.arange(width)
    block_of = (at // COLS // BLOCK) * (COLS // BLOCK) + at % COLS // BLOCK
    block_of = jnp.asarray(block_of[None].astype(np.int32))
    dims = (groups, tiles, mem_dev, slots, band_cells, width, points)
    peers = groups * (2 * HALO + 1) - 1
    f32 = jnp.float32
    vmem = pl.BlockSpec(memory_space=pltpu.VMEM)
    smem = pl.BlockSpec(memory_space=pltpu.SMEM)
    banded = (groups, mem_dev, width)
    square = pltpu.VMEM((members, mpad, points), f32)
    tall = ceil_to(width // LANES * mem_dev, 8)
    dense = pltpu.VMEM((groups, tall, LANES), f32)
    parts = -(-(width // LANES) // 8)
    dma = pltpu.SemaphoreType.DMA
    out = pl.pallas_call(
        functools.partial(kernel, dims),
        out_shape=jax.ShapeDtypeStruct(banded, f32),
        in_specs=[smem, smem] + [vmem] * 5,
        out_specs=vmem,
        scratch_shapes=[
            pltpu.VMEM((mem_dev, slots), f32),
            pltpu.VMEM((3, slots), f32),
            pltpu.VMEM((groups, 2 * HALO + 1, mem_dev, slots), f32),
            pltpu.VMEM((2 * HALO + 1, 3, slots), f32),
            dense, dense, dense, dense,
            pltpu.VMEM((mpad, window), f32),
            pltpu.VMEM((batch * mpad, window), f32),
            square, square, square, square, square,
            pltpu.VMEM((mpad, points), f32),
            dma((peers,)),
            dma((groups, 2 * HALO + 1)),
            dma((2 * HALO + 1,)), dma((2 * HALO + 1,)),
            dma((groups, parts)), dma((groups, parts)),
            dma((groups, parts)), dma((groups, parts)),
        ],
        compiler_params=pltpu.CompilerParams(collective_id=0, has_side_effects=True),
    )(obs_count, radius, bands, obs_index, obs_value, obs_rinv, block_of)
    out = out[:, :, :band_cells].transpose(1, 0, 2)
    return out.reshape(mem_dev, 1, cells)


def solution(mesh):
    in_specs = (
        P("mem", "tile", None),
        P("tile", None),
        P("tile"),
        P("tile", None),
        P("tile", None),
        P("tile"),
    )
    return jax.shard_map(
        functools.partial(shards, mesh.shape["mem"], mesh.shape["tile"]),
        mesh=mesh, in_specs=in_specs, out_specs=P("mem", "tile", None), check_vma=False,
    )
```

```python
import functools
import math

import jax
import jax.numpy as jnp
import numpy as np
from jax import lax
from jax.experimental import pallas as pl
from jax.experimental.pallas import tpu as pltpu
from jax.sharding import PartitionSpec as P

COLS = 45
BLOCK = 9
HALO = 2
NS_ITERS = 4
LANES = 128
MESH = pl.DeviceIdType.MESH


def ceil_to(x, m):
    return (x + m - 1) // m * m


def split(x, parts):
    out = []
    for _ in range(parts):
        piece = x.astype(jnp.bfloat16)
        out.append(piece)
        x = x - piece.astype(jnp.float32)
    return out


def dot(a, b):
    return jnp.dot(a, b, preferred_element_type=jnp.float32)


def dot_nt(a, b):
    return lax.dot_general(a, b, (((1,), (1,)), ((), ())), preferred_element_type=jnp.float32)


def iota(shape, dim):
    return lax.broadcasted_iota(jnp.int32, shape, dim)


def kernel(
    dims,
    count_ref, radius_ref, state_ref, index_ref, value_ref, rinv_ref, block_ref,
    out_ref,
    own_ref, own_meta_ref, obs_ref, meta_ref, st_ref, recv_ref, back_ref, res_ref, pert_ref, prs_ref, gram_ref, y_ref, z_ref, m_ref, t_ref,
    vec_ref, obs_send, obs_recv, meta_send, meta_recv, st_send, st_recv, bk_send, bk_recv,
):
    groups, tiles, mem_dev, slots, band_cells, width, points = dims
    members = groups * mem_dev
    mpad = gram_ref.shape[1]
    rows_dev = band_cells // COLS
    col_blocks = COLS // BLOCK
    me = lax.axis_index("mem")
    tile = lax.axis_index("tile")
    offsets = list(range(-HALO, HALO + 1))
    peers = [(s, d) for d in offsets for s in range(groups) if (s, d) != (0, 0)]

    def member(s):
        return lax.rem(me + s, groups)

    def column(d):
        return lax.rem(tile + d + tiles, tiles)

    barrier = pltpu.get_barrier_semaphore()
    for s, d in peers:
        pl.semaphore_signal(barrier, inc=1, device_id=(member(s), column(d)), device_id_type=MESH)

    cell = index_ref[...]
    cell_f = cell.astype(jnp.float32)
    band = jnp.floor((cell_f + 0.5) * (1.0 / band_cells))
    inside = cell_f - band * band_cells
    strip = jnp.floor((inside + 0.5) * (1.0 / LANES))
    lane = inside - strip * LANES
    strips = width // LANES
    lane_hot = jnp.where(iota((LANES, slots), 0) == lane.astype(jnp.int32), 1.0, 0.0)
    lane_hot = lane_hot.astype(jnp.bfloat16)
    tall = st_ref.shape[1]
    row_strip = iota((tall, 1), 0) // mem_dev
    mine = jnp.where(iota((mem_dev, tall), 1) % mem_dev == iota((mem_dev, tall), 0), 1.0, 0.0)
    mine = mine.astype(jnp.bfloat16)
    own = jnp.zeros((mem_dev, slots), jnp.float32)
    for b in range(groups):
        for r in range(strips):
            first = b * band_cells + r * LANES
            many = min(LANES, band_cells - r * LANES)
            rows = state_ref[:, 0, first : first + many]
            if many < LANES:
                rows = jnp.concatenate([rows, jnp.zeros((mem_dev, LANES - many), jnp.float32)], axis=1)
            st_ref[b, r * mem_dev : (r + 1) * mem_dev] = rows
        if tall > strips * mem_dev:
            st_ref[b, strips * mem_dev :] = jnp.zeros((tall - strips * mem_dev, LANES), jnp.float32)
    for b in range(groups):
        key = jnp.where(band == b, strip, -1.0).astype(jnp.int32)
        hit = row_strip == key
        for part in split(st_ref[b], 3):
            found = jnp.where(hit, dot(part, lane_hot), 0.0)
            own = own + dot(mine, found.astype(jnp.bfloat16))
    live = jnp.where(iota((1, slots), 1) < count_ref[0], rinv_ref[...], 0.0)
    own_ref[...] = own
    obs_ref[me, HALO] = own
    about = jnp.concatenate([value_ref[...], live, cell_f], axis=0)
    own_meta_ref[...] = about
    meta_ref[HALO] = about
    recv_ref[me] = st_ref[me]
    if tall > strips * mem_dev:
        pad = jnp.zeros((groups, tall - strips * mem_dev, LANES), jnp.float32)
        back_ref[:, strips * mem_dev :] = pad

    pl.semaphore_wait(barrier, len(peers))

    def obs_copy(n, s, d):
        return pltpu.make_async_remote_copy(
            src_ref=own_ref,
            dst_ref=obs_ref.at[me, HALO - d],
            send_sem=obs_send.at[n],
            recv_sem=obs_recv.at[me, HALO - d],
            device_id=(member(s), column(d)),
            device_id_type=MESH,
        )

    def obs_wait(n, s, d):
        src = member(s)
        return pltpu.make_async_remote_copy(
            src_ref=own_ref,
            dst_ref=obs_ref.at[src, HALO + d],
            send_sem=obs_send.at[n],
            recv_sem=obs_recv.at[src, HALO + d],
            device_id=(src, column(d)),
            device_id_type=MESH,
        )

    def meta_copy(d, slot, from_tile):
        return pltpu.make_async_remote_copy(
            src_ref=own_meta_ref, dst_ref=meta_ref.at[slot], send_sem=meta_send.at[HALO + d],
            recv_sem=meta_recv.at[slot], device_id=(me, from_tile), device_id_type=MESH,
        )

    per = 2 if strips % 2 == 0 else 1
    chunk = per * LANES
    segments = [(a, min(a + 8, strips)) for a in range(0, strips, 8)]

    def rows_of(i):
        a, b = segments[i]
        first = a * mem_dev
        return pl.ds(first, (tall if b == strips else b * mem_dev) - first)

    def band_copy(s, i, src_ref, dst_ref, send, recv):
        to = member(s)
        return pltpu.make_async_remote_copy(
            src_ref=src_ref.at[to, rows_of(i)], dst_ref=dst_ref.at[me, rows_of(i)],
            send_sem=send.at[s, i], recv_sem=recv.at[me, i],
            device_id=(to, tile), device_id_type=MESH,
        )

    def band_wait(s, i, src_ref, dst_ref, send, recv):
        to = member(s)
        return pltpu.make_async_remote_copy(
            src_ref=src_ref.at[to, rows_of(i)], dst_ref=dst_ref.at[to, rows_of(i)],
            send_sem=send.at[s, i], recv_sem=recv.at[to, i],
            device_id=(to, tile), device_id_type=MESH,
        )

    near = [d for d in offsets if d != 0]
    for d in near:
        meta_copy(d, HALO - d, column(d)).start()

    for n, (s, d) in enumerate(peers):
        obs_copy(n, s, d).start()
    for i in range(len(segments)):
        for s in range(1, groups):
            band_copy(s, i, st_ref, recv_ref, st_send, st_recv).start()
    for d in near:
        meta_copy(d, HALO + d, column(d)).wait_recv()
    for n, (s, d) in enumerate(peers):
        obs_wait(n, s, d).wait_recv()

    point = iota((points, 1), 0).astype(jnp.float32)
    point_row = jnp.floor((point + 0.5) * (1.0 / col_blocks))
    point_col = point - point_row * col_blocks
    half = (BLOCK - 1) // 2
    prow = point_row * BLOCK + (me * rows_dev + half).astype(jnp.float32)
    pcol = point_col * BLOCK + (tile * COLS + half).astype(jnp.float32)
    extent = jnp.full((1, 1), radius_ref[0] * COLS, jnp.int32).astype(jnp.float32)
    circle = float(COLS * tiles)
    weights = []
    for at, d in enumerate(offsets):
        ens = jnp.concatenate([obs_ref[g, at] for g in range(groups)], axis=0)
        meta = meta_ref[at]
        centre = jnp.sum(ens, axis=0, keepdims=True) * (1.0 / members)
        innovation = meta[0:1] - centre
        parts = [ens - centre, innovation]
        if mpad > members + 1:
            parts.append(jnp.zeros((mpad - members - 1, slots), jnp.float32))
        pert_ref[:, at * slots : (at + 1) * slots] = jnp.concatenate(parts, axis=0)
        where = meta[2:3]
        obs_row = jnp.floor((where + 0.5) * (1.0 / COLS))
        obs_col = where - obs_row * COLS + (column(d) * COLS).astype(jnp.float32)
        rgap = jnp.abs(obs_row - prow)
        cgap = jnp.abs(obs_col - pcol)
        cgap = jnp.minimum(cgap, circle - cgap)
        taper = jnp.maximum(0.0, 1.0 - rgap / extent) * jnp.maximum(0.0, 1.0 - cgap / extent)
        weights.append(taper * meta[1:2])
    w_hi, w_lo = split(jnp.concatenate(weights, axis=1), 2)

    batch = prs_ref.shape[0] // mpad

    def gram_group(i, _):
        for k in range(batch):
            prs_ref[k * mpad : (k + 1) * mpad] = pert_ref[pl.ds(i * batch + k, 1)] * pert_ref[...]
        p_hi, p_lo = split(prs_ref[...], 2)
        total = dot_nt(p_hi, w_hi) + dot_nt(p_hi, w_lo) + dot_nt(p_lo, w_hi)
        for k in range(batch):
            gram_ref[i * batch + k] = total[k * mpad : (k + 1) * mpad]
        return 0

    if batch == members:
        gram_group(0, 0)
    else:
        lax.fori_loop(0, members // batch, gram_group, 0)

    full = (members, mpad, points)
    eye = jnp.where(iota((members, mpad, 1), 0) == iota((members, mpad, 1), 1), 1.0, 0.0)
    inside_rows = iota((1, mpad, 1), 1) < members
    g = jnp.where(inside_rows, gram_ref[...], 0.0) + (members - 1.0) * eye
    frob = jnp.sqrt(jnp.sum(jnp.sum(g * g, axis=0), axis=0, keepdims=True))
    y_ref[...] = g / frob[None]
    z_ref[...] = 1.5 * eye - 0.5 * y_ref[...]

    step = 4 if members % 4 == 0 else 1

    def product(a_ref, b_ref, o_ref, finish):
        def body(i, _):
            rows = [i * step + u for u in range(step)]
            acc = [None] * step
            for k in range(members):
                right = b_ref[k]
                for u in range(step):
                    term = a_ref[rows[u], k : k + 1, :] * right
                    acc[u] = term if acc[u] is None else acc[u] + term
            for u in range(step):
                o_ref[rows[u]] = finish(rows[u], acc[u])
            return 0

        lax.fori_loop(0, members // step, body, 0)

    def keep(_, x):
        return x

    def middle(i, x):
        return jnp.where(iota((mpad, 1), 0) == i, 1.5, 0.0) - 0.5 * x

    product(y_ref, z_ref, t_ref, keep)
    y, y_other, z, z_other = t_ref, y_ref, z_ref, None
    spare = [y_other]
    for sweep in range(1, NS_ITERS):
        product(z, y, m_ref, middle)
        if sweep < NS_ITERS - 1:
            new_y = spare.pop()
            product(y, m_ref, new_y, keep)
            old_y = y
            product(m_ref, z, old_y, keep)
            spare.append(z)
            y, z = new_y, old_y
        else:
            new_z = spare.pop()
            product(m_ref, z, new_z, keep)
            z = new_z
    root = z[...] * (1.0 / jnp.sqrt(frob))[None]
    z[...] = root
    inner = sum(z[k] * gram_ref[k, members : members + 1, :] for k in range(members))
    vec_ref[...] = inner
    shift = sum(z[k] * vec_ref[k : k + 1, :] for k in range(members))
    vec_ref[...] = shift
    scale = math.sqrt(members - 1.0)
    for l in range(members):
        z[l] = scale * z[l] + vec_ref[l : l + 1, :]

    def mix_chunk(c, _):
        span = pl.ds(pl.multiple_of(c * chunk, chunk), chunk)
        hot = jnp.where(iota((points, chunk), 0) == block_ref[:, span], 1.0, 0.0).astype(jnp.bfloat16)

        def cells(l):
            q, r = divmod(l, mem_dev)
            rows = [recv_ref[q, pl.ds((c * per + j) * mem_dev + r, 1)] for j in range(per)]
            return jnp.concatenate(rows, axis=1)

        total = sum(cells(l) for l in range(members))
        mean = total * (1.0 / members)
        acc = jnp.broadcast_to(mean, (mpad, chunk))
        for l0 in range(0, members, batch):
            mix = z[l0 : l0 + batch].reshape(batch * mpad, points)
            spread = sum(dot(part, hot) for part in split(mix, 2))
            for l in range(batch):
                dev = cells(l0 + l) - mean
                acc = acc + spread[l * mpad : (l + 1) * mpad] * dev
        for g in range(groups):
            part = acc[g * mem_dev : (g + 1) * mem_dev]
            for j in range(per):
                back_ref[g, pl.ds((c * per + j) * mem_dev, mem_dev)] = part[:, j * LANES : (j + 1) * LANES]
        return 0

    for i, (first, last) in enumerate(segments):
        for s in range(1, groups):
            band_wait(s, i, st_ref, recv_ref, st_send, st_recv).wait_recv()
        lax.fori_loop(first // per, last // per, mix_chunk, 0)
        for s in range(1, groups):
            band_copy(s, i, back_ref, res_ref, bk_send, bk_recv).start()

    res_ref[me] = back_ref[me]
    for n, (s, d) in enumerate(peers):
        obs_copy(n, s, d).wait_send()
    for d in near:
        meta_copy(d, HALO - d, column(d)).wait_send()
    for i in range(len(segments)):
        for s in range(1, groups):
            band_copy(s, i, st_ref, recv_ref, st_send, st_recv).wait_send()
    for i in range(len(segments)):
        for s in range(1, groups):
            band_wait(s, i, back_ref, res_ref, bk_send, bk_recv).wait()
    for b in range(groups):
        for r in range(strips):
            first = b * band_cells + r * LANES
            many = min(LANES, band_cells - r * LANES)
            out_ref[:, 0, first : first + many] = res_ref[b, r * mem_dev : (r + 1) * mem_dev, :many]


def shards(groups, tiles, state, obs_index, obs_count, obs_value, obs_rinv, radius):
    mem_dev, _, cells = state.shape
    slots = obs_index.shape[1]
    members = groups * mem_dev
    band_cells = cells // groups
    width = ceil_to(band_cells, LANES)
    points = (band_cells // COLS // BLOCK) * (COLS // BLOCK)
    mpad = ceil_to(members + 1, 8)
    window = (2 * HALO + 1) * slots
    batch = max(b for b in range(1, members + 1) if members % b == 0 and (b == 1 or b * mpad <= 512))
    at = np.arange(width)
    block_of = (at // COLS // BLOCK) * (COLS // BLOCK) + at % COLS // BLOCK
    block_of = jnp.asarray(block_of[None].astype(np.int32))
    dims = (groups, tiles, mem_dev, slots, band_cells, width, points)
    peers = groups * (2 * HALO + 1) - 1
    f32 = jnp.float32
    vmem = pl.BlockSpec(memory_space=pltpu.VMEM)
    smem = pl.BlockSpec(memory_space=pltpu.SMEM)
    square = pltpu.VMEM((members, mpad, points), f32)
    tall = ceil_to(width // LANES * mem_dev, 8)
    dense = pltpu.VMEM((groups, tall, LANES), f32)
    parts = -(-(width // LANES) // 8)
    dma = pltpu.SemaphoreType.DMA
    out = pl.pallas_call(
        functools.partial(kernel, dims),
        out_shape=jax.ShapeDtypeStruct(state.shape, f32),
        in_specs=[smem, smem] + [vmem] * 5,
        out_specs=vmem,
        scratch_shapes=[
            pltpu.VMEM((mem_dev, slots), f32),
            pltpu.VMEM((3, slots), f32),
            pltpu.VMEM((groups, 2 * HALO + 1, mem_dev, slots), f32),
            pltpu.VMEM((2 * HALO + 1, 3, slots), f32),
            dense, dense, dense, dense,
            pltpu.VMEM((mpad, window), f32),
            pltpu.VMEM((batch * mpad, window), f32),
            square, square, square, square, square,
            pltpu.VMEM((mpad, points), f32),
            dma((peers,)),
            dma((groups, 2 * HALO + 1)),
            dma((2 * HALO + 1,)), dma((2 * HALO + 1,)),
            dma((groups, parts)), dma((groups, parts)),
            dma((groups, parts)), dma((groups, parts)),
        ],
        compiler_params=pltpu.CompilerParams(collective_id=0, has_side_effects=True),
    )(obs_count, radius, state, obs_index, obs_value, obs_rinv, block_of)
    return out.reshape(mem_dev, 1, cells)


def solution(mesh):
    in_specs = (
        P("mem", "tile", None),
        P("tile", None),
        P("tile"),
        P("tile", None),
        P("tile", None),
        P("tile"),
    )
    return jax.shard_map(
        functools.partial(shards, mesh.shape["mem"], mesh.shape["tile"]),
        mesh=mesh, in_specs=in_specs, out_specs=P("mem", "tile", None), check_vma=False,
    )
```
